32 devices in a mesh: pb: 4 (over y, core), col: 8 (over z, x).
Axes of the slice: x: 2, y: 2, z: 4, core: 2. Of those that a mesh axis runs over, the one named last changes fastest.
Arguments:
- queries: bfloat16 [2048, 1024], P(('pb', 'col')), may hold values from -6 to 6
- weights: bfloat16 [128, 512, 1024], P(('pb', 'col')), may hold values from -0.1875 to 0.1875
- shortlist: int32 [2048, 16], P(('pb', 'col')), may hold values from 0 to 127, all different within a row; in each aligned block of 64 rows (0 to 63, 64 to 127, ...) at most 24 rows name the same one
- pos_rank: int32 [2048, 4], P(('pb', 'col')), may hold values from 0 to 15
- pos_label: int32 [2048, 4], P(('pb', 'col')), may hold values from 0 to 511
Outputs:
- grad_weights: bfloat16 [128, 512, 1024], P(('pb', 'col'))
- grad_queries: bfloat16 [2048, 1024], P(('pb', 'col'))
The draws below stay inside these ranges and needn't reach their ends.
Inputs may be any that keep to these rules, and one draw needn't show every extreme that they name: `shortlist`: each row names 16 different clusters. Among the 64 rows of one device no cluster is named more than 24 times, a bound that some block reaches.
All inputs are finite; a program needn't handle non-finite values.
Results may differ from the reference program's by a relative error of at most 0.012.
Values may be sent and summed in bfloat16 or wider, within the bound.
A program may use at most 128 MiB of HBM per device.

```python
import math
import jax
import jax.numpy as jnp
import numpy as np
from jax import lax

D = 1024
CSIZE = 512
K = 16
P_SIZE = 4
Q_DEV = 64
QUERIES = 2048
CLUSTERS = 128
CAP = 24
N_PB = 4
N_COL = 8


def plant(drawn, rng, smallest, largest):
    index_at = [jax.random.randint(jax.random.fold_in(rng, axis), (), 0, length) for axis, length in enumerate(drawn.shape)]
    longest = drawn.shape.index(max(drawn.shape))
    neighbour = index_at[:longest] + [(index_at[longest] + 1) % drawn.shape[longest]] + index_at[longest + 1:]
    return drawn.at[tuple(index_at)].set(smallest).at[tuple(neighbour)].set(largest)


def shard_levels(stream_key, shape, shards, least, top_value):
    def one(position, blocks):
        steps = jax.random.uniform(jax.random.fold_in(jax.random.fold_in(stream_key, 6), position), (blocks,), jnp.float32, least / len(shards), top_value / len(shards))
        return jnp.repeat(jnp.exp(steps), shape[position] // blocks).reshape((-1,) + (1,) * (len(shape) - position - 1))

    loudness = one(*shards[0])
    for cut in shards[1:]:
        loudness = loudness * one(*cut)
    return loudness


def shared_out(key, own, number, rows, number_of, top, limit, lean):
    order = jax.random.permutation(key, number_of)
    heavy_load, usual = load_shares(number_of, rows * top, limit, lean, True), load_shares(number_of, rows * top, limit, lean, False)
    places = jnp.arange(number_of)

    def named(sizes, offset_by):
        used = int((sizes > 0).sum())
        fixed = max(1, used // 4)
        moved = fixed + (places - fixed + offset_by * (used - fixed)) % max(1, number_of - fixed)
        return jnp.zeros((number_of,), jnp.int32).at[order[jnp.where(places < fixed, places, moved)]].set(jnp.asarray(sizes, jnp.int32))

    sizes = jnp.where(number % 4 == 0, named(heavy_load, number // 4), named(usual, number - number // 4 - 1))
    mixed = jax.random.permutation(jax.random.fold_in(own, 3), number_of)
    source_of, taker = mixed[0:number_of // 2 * 2:2], mixed[1:number_of // 2 * 2:2]
    room = jnp.minimum(sizes[source_of] - 1, limit - sizes[taker]) // 2
    room = jnp.where((source_of == order[0]) | (taker == order[0]) | (sizes[taker] == 0), 0, jnp.maximum(room, 0))
    moved = jax.random.randint(jax.random.fold_in(own, 4), (number_of // 2,), 0, 1 << 20) % (room + 1)
    sizes = sizes.at[source_of].add(-moved).at[taker].add(moved)
    items = jnp.searchsorted(jnp.cumsum(sizes), jnp.arange(rows * top), side="right").astype(jnp.int32)
    table = items.reshape(top, rows).T
    table = table[jax.random.permutation(jax.random.fold_in(own, 1), rows)]
    offset_by = jax.random.randint(jax.random.fold_in(own, 2), (rows, 1), 0, top)
    return jnp.take_along_axis(table, (jnp.arange(top)[None, :] + offset_by) % top, axis=1)


def load_shares(number_of, total, most, skew, full):
    weights = [(1 << 20) // math.isqrt(standing ** skew) + 1 for standing in range(1, number_of + 1)]
    largest = most if full else min(most, max(-(-total // number_of), total * weights[0] // sum(weights)))
    least = 1 if total - largest >= number_of - 1 else 0
    counts, rest = [largest] + [least] * (number_of - 1), total - largest - least * (number_of - 1)
    while rest > 0:
        movable = [i for i in range(1, number_of) if counts[i] < largest] or [i for i in range(1, number_of) if counts[i] < most]
        whole, left = sum([weights[i] for i in movable]), rest
        for i in movable:
            more = min(most - counts[i], max(1, left * weights[i] // whole), rest)
            counts[i] = counts[i] + more
            rest = rest - more
    return np.array(counts)


def scatter_about(own_key, dims, spread, bound, cuts=(), kind=jnp.bfloat16):
    result = spread * jax.random.normal(own_key, dims, jnp.float32)
    if cuts:
        result = result * shard_levels(own_key, dims, cuts, -0.22, 0.18)
    return jnp.clip(result, -bound, bound).astype(kind)


def setup_inputs(seed: int = 0) -> dict:
    key_list = jax.random.split(jax.random.key(seed), 6)
    queries = scatter_about(key_list[0], (QUERIES, D), 1.0, 6.0, ((0, 32),))
    weights = scatter_about(key_list[1], (CLUSTERS, CSIZE, D), D ** -0.5, 0.1875, ((0, 32),))
    shortlist_keys = jax.random.split(jax.random.fold_in(key_list[2], 1), QUERIES // Q_DEV)
    shortlist_turns = jax.random.permutation(jax.random.fold_in(key_list[2], 3), QUERIES // Q_DEV)
    shortlist = jax.vmap(lambda own, number: shared_out(jax.random.fold_in(key_list[2], 2), own, number, Q_DEV, CLUSTERS, K, CAP, 2))(shortlist_keys, shortlist_turns).reshape((QUERIES, K))
    pos_rank = plant(jax.random.randint(key_list[3], (QUERIES, P_SIZE), 0, K), jax.random.fold_in(key_list[3], 1), 0, K - 1).astype(jnp.int32)
    pos_label = plant(jax.random.randint(key_list[4], (QUERIES, P_SIZE), 0, CSIZE), jax.random.fold_in(key_list[4], 1), 0, CSIZE - 1).astype(jnp.int32)
    return dict(queries=queries, weights=weights, shortlist=shortlist, pos_rank=pos_rank, pos_label=pos_label)


def reference(queries, weights, shortlist, pos_rank, pos_label):
    total_pairs = QUERIES * K
    clusters_of = shortlist.reshape(-1).astype(jnp.int32)
    pair_ids = jnp.arange(total_pairs, dtype=jnp.int32)
    query_of = (pair_ids // K).astype(jnp.int32)
    rank_of = (pair_ids % K).astype(jnp.int32)
    order = jnp.argsort(clusters_of, stable=True).astype(jnp.int32)
    loads = jnp.bincount(clusters_of, length=CLUSTERS).astype(jnp.int32)
    offsets = (jnp.cumsum(loads) - loads).astype(jnp.int32)
    most_rows = N_PB * N_COL * CAP
    padded_order = jnp.concatenate([order, jnp.zeros((most_rows,), jnp.int32)])
    labels = jnp.arange(CSIZE, dtype=jnp.int32)

    def one_cluster(accum, cluster):
        picks = lax.dynamic_slice(padded_order, (offsets[cluster].astype(jnp.int32),), (most_rows,))
        live = jnp.arange(most_rows, dtype=jnp.int32) < loads[cluster]
        rows_query = query_of[picks]
        rows_rank = rank_of[picks]
        inputs = queries[rows_query].astype(jnp.float32)
        block = weights[cluster].astype(jnp.float32)
        scores = jnp.dot(inputs, block.T, preferred_element_type=jnp.float32)
        target = jnp.zeros(scores.shape, jnp.float32)
        for which in range(P_SIZE):
            same_rank = (pos_rank[rows_query, which] == rows_rank)[:, None]
            same_label = pos_label[rows_query, which][:, None] == labels[None, :]
            target = jnp.maximum(target, jnp.logical_and(same_rank, same_label).astype(jnp.float32))
        grads = jnp.where(live[:, None], jax.nn.sigmoid(scores) - target, 0.0).astype(jnp.bfloat16)
        grads_wide = lax.optimization_barrier(grads).astype(jnp.float32)
        grad_block = jnp.dot(grads_wide.T, inputs, preferred_element_type=jnp.float32).astype(jnp.bfloat16)
        part = jnp.dot(grads_wide, block, preferred_element_type=jnp.float32).astype(jnp.bfloat16)
        part = lax.optimization_barrier(part).astype(jnp.float32)
        accum = accum.at[rows_query].add(jnp.where(live[:, None], part, 0.0))
        return accum, grad_block

    start = jnp.zeros((QUERIES, D), jnp.float32)
    accum, grad_weights = lax.scan(one_cluster, start, jnp.arange(CLUSTERS, dtype=jnp.int32))
    return grad_weights, accum.astype(jnp.bfloat16)
```

```python
import functools

import jax
import jax.numpy as jnp
from jax import lax
from jax.experimental import pallas as pl
from jax.experimental.pallas import tpu as pltpu
from jax.sharding import PartitionSpec as P

META = 128


def query_meta(shortlist, pos_rank, pos_label):
    top_count = shortlist.shape[1]
    rank_ids = lax.broadcasted_iota(jnp.int32, (1, 1, top_count), 2)
    chosen = jnp.sum(jnp.where(pos_rank[:, :, None] == rank_ids, shortlist[:, None, :], 0), axis=2)
    fields = [shortlist // 256, shortlist % 256, chosen // 256, chosen % 256]
    fields += [pos_label // 256, pos_label % 256]
    packed = jnp.concatenate(fields, axis=1)
    packed = jnp.pad(packed, ((0, 0), (0, META - packed.shape[1])))
    return packed.astype(jnp.float32).astype(jnp.bfloat16)


def gradient_block(meta, scores, first_cluster, owned, labels, top_count, positives):
    meta = meta.astype(jnp.float32)
    first = first_cluster.astype(jnp.float32)
    t, p = top_count, positives
    named = meta[:, :t] * 256.0 + meta[:, t : 2 * t] - first
    base = 2 * t
    at_cluster = meta[:, base : base + p] * 256.0 + meta[:, base + p : base + 2 * p] - first
    at_label = meta[:, base + 2 * p : base + 3 * p] * 256.0 + meta[:, base + 3 * p : base + 4 * p]
    places = (at_cluster * labels + at_label).astype(jnp.int32)
    label_ids = lax.broadcasted_iota(jnp.int32, (1, labels), 1)
    columns = []
    for j in range(owned):
        live = jnp.max((named == float(j)).astype(jnp.float32), axis=1, keepdims=True)
        hit = None
        for w in range(p):
            same = (places[:, w : w + 1] - j * labels) == label_ids
            hit = same if hit is None else jnp.logical_or(hit, same)
        part = scores[:, j * labels : (j + 1) * labels]
        sig = 0.5 * jnp.tanh(0.5 * part) + 0.5
        columns.append(((sig - hit.astype(jnp.float32)) * live).astype(jnp.bfloat16))
    return jnp.concatenate(columns, axis=1)


def dense_kernel(owned, labels, top_count, positives, q_ref, m_ref, w_ref, gw_ref, part_ref, acc):
    step = pl.program_id(0)
    me = lax.axis_index("pb") * lax.axis_size("col") + lax.axis_index("col")

    @pl.when(step == 0)
    def _():
        acc[...] = jnp.zeros_like(acc)

    q = q_ref[...]
    scores = lax.dot_general(q, w_ref[...], (((1,), (1,)), ((), ())), preferred_element_type=jnp.float32)
    g = gradient_block(m_ref[...], scores, me * owned, owned, labels, top_count, positives)
    part_ref[...] = jnp.dot(g, w_ref[...], preferred_element_type=jnp.float32).astype(jnp.bfloat16)
    acc[...] += lax.dot_general(g, q, (((0,), (0,)), ((), ())), preferred_element_type=jnp.float32)

    @pl.when(step == pl.num_programs(0) - 1)
    def _():
        gw_ref[...] = acc[...].astype(jnp.bfloat16)


def body(queries, weights, shortlist, pos_rank, pos_label):
    rows, width = queries.shape
    owned, labels, _ = weights.shape
    pb_count, col_count = lax.axis_size("pb"), lax.axis_size("col")
    devices = pb_count * col_count
    sent = jnp.concatenate([queries, query_meta(shortlist, pos_rank, pos_label)], axis=1)
    everyone = lax.all_gather(sent, ("pb", "col"), axis=0, tiled=True)
    total = devices * rows
    block = 256
    grad_weights, part = pl.pallas_call(
        functools.partial(dense_kernel, owned, labels, shortlist.shape[1], pos_rank.shape[1]),
        grid=(total // block,),
        in_specs=[
            pl.BlockSpec((block, width), lambda i: (i, 0)),
            pl.BlockSpec((block, META), lambda i: (i, width // META)),
            pl.BlockSpec((owned * labels, width), lambda i: (0, 0)),
        ],
        out_specs=[
            pl.BlockSpec((owned * labels, width), lambda i: (0, 0)),
            pl.BlockSpec((block, width), lambda i: (i, 0)),
        ],
        out_shape=[
            jax.ShapeDtypeStruct((owned * labels, width), jnp.bfloat16),
            jax.ShapeDtypeStruct((total, width), jnp.bfloat16),
        ],
        scratch_shapes=[pltpu.VMEM((owned * labels, width), jnp.float32)],
        compiler_params=pltpu.CompilerParams(vmem_limit_bytes=60 * 1024 * 1024),
    )(everyone, everyone, weights.reshape(owned * labels, width))
    part = part.reshape(pb_count, col_count, rows, width)
    part = lax.all_to_all(part, "pb", split_axis=0, concat_axis=0, tiled=True)
    part = jnp.sum(part, axis=0, dtype=jnp.float32).astype(jnp.bfloat16)
    part = lax.all_to_all(part, "col", split_axis=0, concat_axis=0, tiled=True)
    grad_queries = jnp.sum(part, axis=0, dtype=jnp.float32).astype(jnp.bfloat16)
    return grad_weights.reshape(weights.shape), grad_queries


def solution(mesh):
    return jax.shard_map(
        body,
        mesh=mesh,
        in_specs=(
            P(("pb", "col"), None),
            P(("pb", "col"), None, None),
            P(("pb", "col"), None),
            P(("pb", "col"), None),
            P(("pb", "col"), None),
        ),
        out_specs=(P(("pb", "col"), None, None), P(("pb", "col"), None)),
        check_vma=False,
    )
```

```python
import functools

import jax
import jax.numpy as jnp
from jax import lax
from jax.experimental import pallas as pl
from jax.experimental.pallas import tpu as pltpu
from jax.sharding import PartitionSpec as P

META = 128


def query_meta(shortlist, pos_rank, pos_label):
    top_count = shortlist.shape[1]
    rank_ids = lax.broadcasted_iota(jnp.int32, (1, 1, top_count), 2)
    chosen = jnp.sum(jnp.where(pos_rank[:, :, None] == rank_ids, shortlist[:, None, :], 0), axis=2)
    fields = [shortlist // 256, shortlist % 256, chosen // 256, chosen % 256]
    fields += [pos_label // 256, pos_label % 256]
    packed = jnp.concatenate(fields, axis=1)
    packed = jnp.pad(packed, ((0, 0), (0, META - packed.shape[1])))
    return packed.astype(jnp.float32).astype(jnp.bfloat16)


def gradient_block(meta, scores, first_cluster, owned, labels, top_count, positives):
    meta = meta.astype(jnp.float32)
    first = first_cluster.astype(jnp.float32)
    t, p = top_count, positives
    named = meta[:, :t] * 256.0 + meta[:, t : 2 * t] - first
    base = 2 * t
    at_cluster = meta[:, base : base + p] * 256.0 + meta[:, base + p : base + 2 * p] - first
    at_label = meta[:, base + 2 * p : base + 3 * p] * 256.0 + meta[:, base + 3 * p : base + 4 * p]
    places = (at_cluster * labels + at_label).astype(jnp.int32)
    label_ids = lax.broadcasted_iota(jnp.int32, (1, labels), 1)
    columns = []
    for j in range(owned):
        live = jnp.max((named == float(j)).astype(jnp.float32), axis=1, keepdims=True)
        hit = None
        for w in range(p):
            same = (places[:, w : w + 1] - j * labels) == label_ids
            hit = same if hit is None else jnp.logical_or(hit, same)
        part = scores[:, j * labels : (j + 1) * labels]
        sig = 0.5 * jnp.tanh(0.5 * part) + 0.5
        columns.append(((sig - hit.astype(jnp.float32)) * live).astype(jnp.bfloat16))
    return jnp.concatenate(columns, axis=1)


def dense_kernel(owned, labels, top_count, positives, q_ref, m_ref, w_ref, gw_ref, part_ref, acc):
    step = pl.program_id(0)
    me = lax.axis_index("pb") * lax.axis_size("col") + lax.axis_index("col")

    @pl.when(step == 0)
    def _():
        acc[...] = jnp.zeros_like(acc)

    q = q_ref[...]
    scores = lax.dot_general(q, w_ref[...], (((1,), (1,)), ((), ())), preferred_element_type=jnp.float32)
    g = gradient_block(m_ref[...], scores, me * owned, owned, labels, top_count, positives)
    part_ref[...] = jnp.dot(g, w_ref[...], preferred_element_type=jnp.float32).astype(jnp.bfloat16)
    acc[...] += lax.dot_general(g, q, (((0,), (0,)), ((), ())), preferred_element_type=jnp.float32)

    @pl.when(step == pl.num_programs(0) - 1)
    def _():
        gw_ref[...] = acc[...].astype(jnp.bfloat16)


OWN, PAIR, NEAR_A, NEAR_B, PAIR_NEAR_A, PAIR_NEAR_B, FAR, PAIR_FAR = 0, 1, 2, 3, 5, 4, 6, 7
ZS = 4


def routed_kernel(
    owned,
    labels,
    top_count,
    positives,
    sent_ref,
    w_hbm,
    gw_hbm,
    gq_ref,
    w_ref,
    qbuf,
    gbuf,
    part,
    from_pair,
    from_b,
    from_a,
    from_z,
    gwbuf,
    send_sem,
    recv_sem,
    w_sem,
    out_sem,
):
    rows, _ = sent_ref.shape
    width = w_ref.shape[1]
    pb, col = lax.axis_index("pb"), lax.axis_index("col")
    y, core = pb // 2, pb % 2
    z, x = col // 2, col % 2
    pair = (y * 2 + (1 - core), col)
    xa = x + (1 - core) * (1 - 2 * x)
    ya = y + core * (1 - 2 * y)
    xb = x + core * (1 - 2 * x)
    yb = y + (1 - core) * (1 - 2 * y)
    side_a = (ya * 2 + core, z * 2 + xa)
    side_b = (yb * 2 + core, z * 2 + xb)
    z_peers = [None] + [(pb, ((z + k) % ZS) * 2 + x) for k in range(1, ZS)]
    z_rows = [pl.ds(pl.multiple_of(((z + ZS - k) % ZS) * rows, rows), rows) for k in range(ZS)]
    z_goals = [pl.ds(pl.multiple_of(((z + k) % ZS) * rows, rows), rows) for k in range(ZS)]

    load_w = pltpu.make_async_copy(w_hbm, w_ref, w_sem)
    load_w.start()

    barrier = pltpu.get_barrier_semaphore()
    for peer in z_peers[1:] + [side_a, side_b, pair]:
        pl.semaphore_signal(barrier, inc=1, device_id=peer, device_id_type=pl.DeviceIdType.MESH)
    pl.semaphore_wait(barrier, ZS + 2)

    def copy(index, src, dst, peer):
        return pltpu.make_async_remote_copy(
            src_ref=src,
            dst_ref=dst,
            send_sem=send_sem.at[index],
            recv_sem=recv_sem.at[index],
            device_id=peer,
            device_id_type=pl.DeviceIdType.MESH,
        )

    def chunk(slot, k):
        return qbuf.at[slot, z_rows[k]]

    z_copies = [None] + [copy(k, sent_ref, chunk(OWN, 0), z_peers[k]) for k in range(1, ZS)]
    z_arrivals = [None] + [copy(k, sent_ref, chunk(OWN, k), z_peers[k]) for k in range(1, ZS)]

    def source(slot, k):
        return sent_ref if slot == OWN and k == 0 else chunk(slot, k)

    def hops(base, from_slot, to_slot, peer):
        return [copy(base + k, source(from_slot, k), chunk(to_slot, k), peer) for k in range(ZS)]

    own_a = hops(4, OWN, NEAR_A, side_a)
    own_b = hops(8, OWN, NEAR_B, side_b)
    own_pair = hops(12, OWN, PAIR, pair)
    a_b = hops(16, NEAR_A, FAR, side_b)
    a_pair = hops(20, NEAR_A, PAIR_NEAR_B, pair)
    b_pair = hops(24, NEAR_B, PAIR_NEAR_A, pair)
    far_pair = hops(28, FAR, PAIR_FAR, pair)

    for k in range(1, ZS):
        z_copies[k].start()
    own_a[0].start()
    own_b[0].start()
    own_pair[0].start()
    qbuf[OWN, z_rows[0], :] = sent_ref[...]

    def relay_z(k):
        z_arrivals[k].wait_recv()
        own_a[k].start()
        own_b[k].start()
        own_pair[k].start()

    def relay_a(k):
        own_a[k].wait_recv()
        a_b[k].start()
        a_pair[k].start()

    relay_z(1)
    relay_a(0)
    relay_z(3)
    relay_a(1)
    relay_z(2)
    load_w.wait()

    first = (pb * lax.axis_size("col") + col) * owned

    def score_step(s, _):
        @pl.when(s == PAIR)
        def _():
            for k in range(ZS):
                own_pair[k].wait_recv()
            relay_a(3)

        @pl.when(s == NEAR_A)
        def _():
            relay_a(2)

        @pl.when(s == NEAR_B)
        def _():
            for k in range(ZS):
                own_b[k].wait_recv()
                b_pair[k].start()

        @pl.when(s == PAIR_NEAR_B)
        def _():
            for k in range(ZS):
                a_pair[k].wait_recv()

        @pl.when(s == PAIR_NEAR_A)
        def _():
            for k in range(ZS):
                b_pair[k].wait_recv()

        @pl.when(s == FAR)
        def _():
            for k in range(ZS):
                a_b[k].wait_recv()
                far_pair[k].start()

        @pl.when(s == PAIR_FAR)
        def _():
            for k in range(ZS):
                far_pair[k].wait_recv()

        scores = lax.dot_general(
            qbuf[s, :, :width], w_ref[...], (((1,), (1,)), ((), ())), preferred_element_type=jnp.float32
        )
        gbuf[s] = gradient_block(
            qbuf[s, :, width:], scores, first, owned, labels, top_count, positives
        )
        return 0

    lax.fori_loop(0, 8, score_step, 0)

    back_pair = {
        PAIR_FAR: copy(32, part.at[PAIR_FAR], from_pair.at[0], pair),
        PAIR_NEAR_A: copy(33, part.at[PAIR_NEAR_A], from_pair.at[1], pair),
        PAIR_NEAR_B: copy(34, part.at[PAIR_NEAR_B], from_pair.at[2], pair),
        PAIR: copy(35, part.at[PAIR], from_pair.at[3], pair),
    }
    back_far = copy(36, part.at[FAR], from_b.at[0], side_b)
    back_b = copy(37, part.at[NEAR_B], from_b.at[1], side_b)
    back_a = copy(38, part.at[NEAR_A], from_a, side_a)
    back_z = [None] + [
        copy(38 + k, part.at[OWN, z_goals[k]], from_z.at[k - 1], z_peers[k]) for k in range(1, ZS)
    ]

    def add_to(slot, *arrived):
        total = part[slot].astype(jnp.float32)
        for ref in arrived:
            total = total + ref[...].astype(jnp.float32)
        part[slot] = total.astype(jnp.bfloat16)

    def part_step(t, _):
        slot = 7 - t
        part[slot] = jnp.dot(gbuf[slot], w_ref[...], preferred_element_type=jnp.float32).astype(
            jnp.bfloat16
        )
        for which, back in back_pair.items():

            @pl.when(slot == which)
            def _():
                back.start()

        @pl.when(slot == 5)
        def _():
            back_pair[PAIR_FAR].wait_recv()
            add_to(FAR, from_pair.at[0])
            back_far.start()

        @pl.when(slot == 3)
        def _():
            back_pair[PAIR_NEAR_A].wait_recv()
            add_to(NEAR_B, from_pair.at[1])
            back_b.start()

        @pl.when(slot == 1)
        def _():
            back_pair[PAIR_NEAR_B].wait_recv()
            back_far.wait_recv()
            add_to(NEAR_A, from_pair.at[2], from_b.at[0])
            back_a.start()

        return 0

    lax.fori_loop(0, 8, part_step, 0)

    tile = labels // 2

    def out_copy(u):
        return pltpu.make_async_copy(
            gwbuf.at[u], gw_hbm.at[pl.ds(pl.multiple_of(u * tile, tile), tile)], out_sem.at[u]
        )

    def weight_step(u, _):
        columns = pl.ds(pl.multiple_of(u * tile, tile), tile)
        g = gbuf[:, :, columns].reshape(-1, tile)
        q = qbuf[:, :, :width].reshape(-1, width)
        gwbuf[u] = lax.dot_general(
            g, q, (((0,), (0,)), ((), ())), preferred_element_type=jnp.float32
        ).astype(jnp.bfloat16)
        out_copy(u).start()

        @pl.when(u == 2)
        def _():
            back_pair[PAIR].wait_recv()
            back_b.wait_recv()
            back_a.wait_recv()
            add_to(OWN, from_pair.at[3], from_b.at[1], from_a)
            for k in range(1, ZS):
                back_z[k].start()

        return 0

    count = owned * labels // tile
    lax.fori_loop(0, count, weight_step, 0)

    total = part[OWN, z_rows[0], :].astype(jnp.float32)
    for k in range(1, ZS):
        back_z[k].wait_recv()
        total = total + from_z[k - 1].astype(jnp.float32)
    gq_ref[...] = total.astype(jnp.bfloat16)

    everything = z_copies[1:] + own_a + own_b + own_pair + a_b + a_pair + b_pair + far_pair
    everything += list(back_pair.values()) + [back_far, back_b, back_a] + back_z[1:]
    for one in everything:
        one.wait_send()
    for u in range(count):
        out_copy(u).wait()


def routed(sent, weights, top_count, positives):
    rows, packed = sent.shape
    owned, labels, width = weights.shape
    block = ZS * rows
    count = owned * labels // (labels // 2)
    bf16 = jnp.bfloat16
    return pl.pallas_call(
        functools.partial(routed_kernel, owned, labels, top_count, positives),
        in_specs=[
            pl.BlockSpec(memory_space=pltpu.VMEM),
            pl.BlockSpec(memory_space=pl.ANY),
        ],
        out_specs=[
            pl.BlockSpec(memory_space=pl.ANY),
            pl.BlockSpec(memory_space=pltpu.VMEM),
        ],
        out_shape=[
            jax.ShapeDtypeStruct((owned * labels, width), bf16),
            jax.ShapeDtypeStruct((rows, width), bf16),
        ],
        scratch_shapes=[
            pltpu.VMEM((owned * labels, width), bf16),
            pltpu.VMEM((8, block, packed), bf16),
            pltpu.VMEM((8, block, owned * labels), bf16),
            pltpu.VMEM((8, block, width), bf16),
            pltpu.VMEM((4, block, width), bf16),
            pltpu.VMEM((2, block, width), bf16),
            pltpu.VMEM((block, width), bf16),
            pltpu.VMEM((ZS - 1, rows, width), bf16),
            pltpu.VMEM((count, labels // 2, width), bf16),
            pltpu.SemaphoreType.DMA((42,)),
            pltpu.SemaphoreType.DMA((42,)),
            pltpu.SemaphoreType.DMA,
            pltpu.SemaphoreType.DMA((count,)),
        ],
        compiler_params=pltpu.CompilerParams(
            collective_id=0, has_side_effects=True, vmem_limit_bytes=60 * 1024 * 1024
        ),
    )(sent, weights.reshape(owned * labels, width))


def body(queries, weights, shortlist, pos_rank, pos_label):
    rows, width = queries.shape
    owned, labels, _ = weights.shape
    pb_count, col_count = lax.axis_size("pb"), lax.axis_size("col")
    devices = pb_count * col_count
    sent = jnp.concatenate([queries, query_meta(shortlist, pos_rank, pos_label)], axis=1)
    if (pb_count, col_count) == (4, 2 * ZS):
        grad_weights, grad_queries = routed(sent, weights, shortlist.shape[1], pos_rank.shape[1])
        return grad_weights.reshape(weights.shape), grad_queries
    everyone = lax.all_gather(sent, ("pb", "col"), axis=0, tiled=True)
    total = devices * rows
    block = 256
    grad_weights, part = pl.pallas_call(
        functools.partial(dense_kernel, owned, labels, shortlist.shape[1], pos_rank.shape[1]),
        grid=(total // block,),
        in_specs=[
            pl.BlockSpec((block, width), lambda i: (i, 0)),
            pl.BlockSpec((block, META), lambda i: (i, width // META)),
            pl.BlockSpec((owned * labels, width), lambda i: (0, 0)),
        ],
        out_specs=[
            pl.BlockSpec((owned * labels, width), lambda i: (0, 0)),
            pl.BlockSpec((block, width), lambda i: (i, 0)),
        ],
        out_shape=[
            jax.ShapeDtypeStruct((owned * labels, width), jnp.bfloat16),
            jax.ShapeDtypeStruct((total, width), jnp.bfloat16),
        ],
        scratch_shapes=[pltpu.VMEM((owned * labels, width), jnp.float32)],
        compiler_params=pltpu.CompilerParams(vmem_limit_bytes=60 * 1024 * 1024),
    )(everyone, everyone, weights.reshape(owned * labels, width))
    part = part.reshape(pb_count, col_count, rows, width)
    part = lax.all_to_all(part, "pb", split_axis=0, concat_axis=0, tiled=True)
    part = jnp.sum(part, axis=0, dtype=jnp.float32).astype(jnp.bfloat16)
    part = lax.all_to_all(part, "col", split_axis=0, concat_axis=0, tiled=True)
    grad_queries = jnp.sum(part, axis=0, dtype=jnp.float32).astype(jnp.bfloat16)
    return grad_weights.reshape(weights.shape), grad_queries


def solution(mesh):
    return jax.shard_map(
        body,
        mesh=mesh,
        in_specs=(
            P(("pb", "col"), None),
            P(("pb", "col"), None, None),
            P(("pb", "col"), None),
            P(("pb", "col"), None),
            P(("pb", "col"), None),
        ),
        out_specs=(P(("pb", "col"), None, None), P(("pb", "col"), None)),
        check_vma=False,
    )
```

```python
import functools

import jax
import jax.numpy as jnp
from jax import lax
from jax.experimental import pallas as pl
from jax.experimental.pallas import tpu as pltpu
from jax.sharding import PartitionSpec as P

META = 128


def query_meta(shortlist, pos_rank, pos_label):
    top_count = shortlist.shape[1]
    rank_ids = lax.broadcasted_iota(jnp.int32, (1, 1, top_count), 2)
    chosen = jnp.sum(jnp.where(pos_rank[:, :, None] == rank_ids, shortlist[:, None, :], 0), axis=2)
    fields = [shortlist // 256, shortlist % 256, chosen // 256, chosen % 256]
    fields += [pos_label // 256, pos_label % 256]
    packed = jnp.concatenate(fields, axis=1)
    packed = jnp.pad(packed, ((0, 0), (0, META - packed.shape[1])))
    return packed.astype(jnp.float32).astype(jnp.bfloat16)


def gradient_block(meta, scores, first_cluster, owned, labels, top_count, positives):
    meta = meta.astype(jnp.float32)
    first = first_cluster.astype(jnp.float32)
    t, p = top_count, positives
    named = meta[:, :t] * 256.0 + meta[:, t : 2 * t] - first
    base = 2 * t
    at_cluster = meta[:, base : base + p] * 256.0 + meta[:, base + p : base + 2 * p] - first
    at_label = meta[:, base + 2 * p : base + 3 * p] * 256.0 + meta[:, base + 3 * p : base + 4 * p]
    places = (at_cluster * labels + at_label).astype(jnp.int32)
    label_ids = lax.broadcasted_iota(jnp.int32, (1, labels), 1)
    columns = []
    for j in range(owned):
        live = jnp.max((named == float(j)).astype(jnp.float32), axis=1, keepdims=True)
        hit = None
        for w in range(p):
            same = (places[:, w : w + 1] - j * labels) == label_ids
            hit = same if hit is None else jnp.logical_or(hit, same)
        part = scores[:, j * labels : (j + 1) * labels]
        sig = 0.5 * jnp.tanh(0.5 * part) + 0.5
        columns.append(((sig - hit.astype(jnp.float32)) * live).astype(jnp.bfloat16))
    return jnp.concatenate(columns, axis=1)


def dense_kernel(owned, labels, top_count, positives, q_ref, m_ref, w_ref, gw_ref, part_ref, acc):
    step = pl.program_id(0)
    me = lax.axis_index("pb") * lax.axis_size("col") + lax.axis_index("col")

    @pl.when(step == 0)
    def _():
        acc[...] = jnp.zeros_like(acc)

    q = q_ref[...]
    scores = lax.dot_general(q, w_ref[...], (((1,), (1,)), ((), ())), preferred_element_type=jnp.float32)
    g = gradient_block(m_ref[...], scores, me * owned, owned, labels, top_count, positives)
    part_ref[...] = jnp.dot(g, w_ref[...], preferred_element_type=jnp.float32).astype(jnp.bfloat16)
    acc[...] += lax.dot_general(g, q, (((0,), (0,)), ((), ())), preferred_element_type=jnp.float32)

    @pl.when(step == pl.num_programs(0) - 1)
    def _():
        gw_ref[...] = acc[...].astype(jnp.bfloat16)


OWN, PAIR, NEAR_A, NEAR_B, PAIR_NEAR_A, PAIR_NEAR_B, FAR, PAIR_FAR = 0, 1, 2, 3, 5, 4, 6, 7
ZS = 4


def packed_meta(short_ref, rank_ref, label_ref):
    short, ranks, places = short_ref[...], rank_ref[...], label_ref[...]
    top_count, rows = short.shape
    count = ranks.shape[0]
    standing = lax.broadcasted_iota(jnp.int32, short.shape, 0)
    lines = []
    for w in range(count):
        mine = jnp.where(standing == ranks[w : w + 1], short, 0)
        lines.append(jnp.sum(mine, axis=0, keepdims=True))
    lines = [v >> 8 for v in lines] + [v & 255 for v in lines]
    lines += [places[w : w + 1] >> 8 for w in range(count)]
    lines += [places[w : w + 1] & 255 for w in range(count)]
    extra_ids = lax.broadcasted_iota(jnp.int32, (len(lines), rows), 0)
    extra = jnp.zeros((len(lines), rows), jnp.int32)
    for i, line in enumerate(lines):
        extra = jnp.where(extra_ids == i, line, extra)
    rest = jnp.zeros((META - 2 * top_count - len(lines), rows), jnp.int32)
    fields = jnp.concatenate([short >> 8, short & 255, extra, rest], axis=0)
    row_ids = lax.broadcasted_iota(jnp.int32, (rows, rows), 0)
    col_ids = lax.broadcasted_iota(jnp.int32, (rows, rows), 1)
    same = (row_ids == col_ids).astype(jnp.float32).astype(jnp.bfloat16)
    return lax.dot_general(
        same,
        fields.astype(jnp.float32).astype(jnp.bfloat16),
        (((1,), (1,)), ((), ())),
        preferred_element_type=jnp.float32,
    ).astype(jnp.bfloat16)


def routed_kernel(
    owned,
    labels,
    top_count,
    positives,
    q_ref,
    short_ref,
    rank_ref,
    label_ref,
    w_hbm,
    gw_hbm,
    gq_ref,
    w_ref,
    qbuf,
    gbuf,
    part,
    from_pair,
    from_b,
    from_a,
    from_z,
    gwbuf,
    send_sem,
    recv_sem,
    w_sem,
    out_sem,
):
    rows, width = q_ref.shape
    pb, col = lax.axis_index("pb"), lax.axis_index("col")
    y, core = pb // 2, pb % 2
    z, x = col // 2, col % 2
    pair = (y * 2 + (1 - core), col)
    xa = x + (1 - core) * (1 - 2 * x)
    ya = y + core * (1 - 2 * y)
    xb = x + core * (1 - 2 * x)
    yb = y + (1 - core) * (1 - 2 * y)
    side_a = (ya * 2 + core, z * 2 + xa)
    side_b = (yb * 2 + core, z * 2 + xb)
    z_of = [z, z + 1 - 2 * (z % 2), (z + 2) % ZS, ZS - 1 - z]
    z_peers = [(pb, zk * 2 + x) for zk in z_of]
    z_rows = [pl.ds(pl.multiple_of(zk * rows, rows), rows) for zk in z_of]

    load_w = pltpu.make_async_copy(w_hbm, w_ref, w_sem)
    load_w.start()

    barrier = pltpu.get_barrier_semaphore()
    for peer in z_peers[1:] + [side_a, side_b, pair]:
        pl.semaphore_signal(barrier, inc=1, device_id=peer, device_id_type=pl.DeviceIdType.MESH)
    qbuf[OWN, z_rows[0], :width] = q_ref[...]
    qbuf[OWN, z_rows[0], width:] = packed_meta(short_ref, rank_ref, label_ref)
    pl.semaphore_wait(barrier, ZS + 2)

    def copy(index, src, dst, peer):
        return pltpu.make_async_remote_copy(
            src_ref=src,
            dst_ref=dst,
            send_sem=send_sem.at[index],
            recv_sem=recv_sem.at[index],
            device_id=peer,
            device_id_type=pl.DeviceIdType.MESH,
        )

    def chunk(slot, k):
        return qbuf.at[slot, z_rows[k]]

    z_copies = [None] + [
        copy(k, chunk(OWN, 0), chunk(OWN, 0), z_peers[k]) for k in range(1, ZS)
    ]
    z_arrivals = [None] + [
        copy(k, chunk(OWN, 0), chunk(OWN, k), z_peers[k]) for k in range(1, ZS)
    ]

    def hops(base, from_slot, to_slot, peer):
        return [copy(base + k, chunk(from_slot, k), chunk(to_slot, k), peer) for k in range(ZS)]

    own_a = hops(4, OWN, NEAR_A, side_a)
    own_b = hops(8, OWN, NEAR_B, side_b)
    own_pair = hops(12, OWN, PAIR, pair)
    a_b = hops(16, NEAR_A, FAR, side_b)
    a_pair = hops(20, NEAR_A, PAIR_NEAR_B, pair)
    b_pair = hops(24, NEAR_B, PAIR_NEAR_A, pair)
    far_pair = hops(28, FAR, PAIR_FAR, pair)

    for k in (1, 3, 2):
        z_copies[k].start()
    own_a[0].start()
    own_b[0].start()
    own_pair[0].start()

    def relay_z(k):
        z_arrivals[k].wait_recv()
        own_a[k].start()
        own_b[k].start()
        own_pair[k].start()

    def relay_a(k):
        own_a[k].wait_recv()
        a_b[k].start()
        a_pair[k].start()

    relay_z(1)
    relay_a(0)
    relay_z(3)
    relay_a(1)
    relay_z(2)
    load_w.wait()

    first = (pb * lax.axis_size("col") + col) * owned

    halves = [pl.ds(h * (width // 2), width // 2) for h in range(2)]
    back_pair = {
        PAIR_FAR: copy(32, part.at[PAIR_FAR], from_pair.at[0], pair),
        PAIR_NEAR_A: copy(33, part.at[PAIR_NEAR_A], from_pair.at[1], pair),
        PAIR_NEAR_B: copy(34, part.at[PAIR_NEAR_B], from_pair.at[2], pair),
        PAIR: copy(35, part.at[PAIR], from_pair.at[3], pair),
    }
    back_b = copy(36, part.at[NEAR_B], from_b.at[1], side_b)
    back_far = [
        copy(37 + h, part.at[FAR, :, halves[h]], from_b.at[0, :, halves[h]], side_b)
        for h in range(2)
    ]
    back_a = [
        copy(39 + h, part.at[NEAR_A, :, halves[h]], from_a.at[:, halves[h]], side_a)
        for h in range(2)
    ]
    back_z = [
        [
            copy(
                41 + 3 * h + k - 1,
                part.at[OWN, z_rows[k], halves[h]],
                from_z.at[k - 1, :, halves[h]],
                z_peers[k],
            )
            for k in (1, 3, 2)
        ]
        for h in range(2)
    ]

    def add_to(slot, columns, *arrived):
        total = part[slot, :, columns].astype(jnp.float32)
        for ref in arrived:
            total = total + ref[:, columns].astype(jnp.float32)
        part[slot, :, columns] = total.astype(jnp.bfloat16)

    def score_step(s, _):
        @pl.when(s == PAIR)
        def _():
            for k in range(ZS):
                own_pair[k].wait_recv()
            relay_a(3)

        @pl.when(s == NEAR_A)
        def _():
            relay_a(2)

        @pl.when(s == NEAR_B)
        def _():
            for k in range(ZS):
                own_b[k].wait_recv()
                b_pair[k].start()

        @pl.when(s == PAIR_NEAR_B)
        def _():
            for k in range(ZS):
                a_pair[k].wait_recv()

        @pl.when(s == PAIR_NEAR_A)
        def _():
            for k in range(ZS):
                b_pair[k].wait_recv()

        @pl.when(s == FAR)
        def _():
            for k in range(ZS):
                a_b[k].wait_recv()
                far_pair[k].start()

        @pl.when(s == PAIR_FAR)
        def _():
            for k in range(ZS):
                far_pair[k].wait_recv()

        scores = lax.dot_general(
            qbuf[s, :, :width], w_ref[...], (((1,), (1,)), ((), ())), preferred_element_type=jnp.float32
        )
        g = gradient_block(qbuf[s, :, width:], scores, first, owned, labels, top_count, positives)
        gbuf[s] = g
        part[s] = jnp.dot(g, w_ref[...], preferred_element_type=jnp.float32).astype(jnp.bfloat16)
        for which, back in back_pair.items():

            @pl.when(s == which)
            def _():
                back.start()

        @pl.when(s == FAR)
        def _():
            back_pair[PAIR_NEAR_A].wait_recv()
            add_to(NEAR_B, pl.ds(0, width), from_pair.at[1])
            back_b.start()

        return 0

    lax.fori_loop(0, 8, score_step, 0)

    tile = labels // 2

    def out_copy(u):
        return pltpu.make_async_copy(
            gwbuf.at[u], gw_hbm.at[pl.ds(pl.multiple_of(u * tile, tile), tile)], out_sem.at[u]
        )

    def weight_step(u, _):
        columns = pl.ds(pl.multiple_of(u * tile, tile), tile)
        g = gbuf[:, :, columns].reshape(-1, tile)
        q = qbuf[:, :, :width].reshape(-1, width)
        gwbuf[u] = lax.dot_general(
            g, q, (((0,), (0,)), ((), ())), preferred_element_type=jnp.float32
        ).astype(jnp.bfloat16)
        out_copy(u).start()

        @pl.when(u == 0)
        def _():
            back_pair[PAIR_FAR].wait_recv()
            for h in range(2):
                add_to(FAR, halves[h], from_pair.at[0])
                back_far[h].start()
            back_pair[PAIR_NEAR_B].wait_recv()

        for h in range(2):

            @pl.when(u == 2 + h)
            def _():
                back_far[h].wait_recv()
                add_to(NEAR_A, halves[h], from_pair.at[2], from_b.at[0])
                back_a[h].start()

            @pl.when(u == 4 + h)
            def _():
                if h == 0:
                    back_pair[PAIR].wait_recv()
                    back_b.wait_recv()
                back_a[h].wait_recv()
                add_to(OWN, halves[h], from_pair.at[3], from_b.at[1], from_a)
                for one in back_z[h]:
                    one.start()

        return 0

    count = owned * labels // tile
    lax.fori_loop(0, count, weight_step, 0)

    for h in range(2):
        total = part[OWN, z_rows[0], halves[h]].astype(jnp.float32)
        for one in back_z[h]:
            one.wait_recv()
        for k in range(ZS - 1):
            total = total + from_z[k, :, halves[h]].astype(jnp.float32)
        gq_ref[:, halves[h]] = total.astype(jnp.bfloat16)

    everything = z_copies[1:] + own_a + own_b + own_pair + a_b + a_pair + b_pair + far_pair
    everything += list(back_pair.values()) + [back_b] + back_far + back_a + back_z[0] + back_z[1]
    for one in everything:
        one.wait_send()
    for u in range(count):
        out_copy(u).wait()


def routed(queries, weights, shortlist, pos_rank, pos_label):
    rows = queries.shape[0]
    packed = queries.shape[1] + META
    top_count, positives = shortlist.shape[1], pos_rank.shape[1]
    owned, labels, width = weights.shape
    block = ZS * rows
    count = owned * labels // (labels // 2)
    bf16 = jnp.bfloat16
    return pl.pallas_call(
        functools.partial(routed_kernel, owned, labels, top_count, positives),
        in_specs=[pl.BlockSpec(memory_space=pltpu.VMEM)] * 4
        + [pl.BlockSpec(memory_space=pl.ANY)],
        out_specs=[
            pl.BlockSpec(memory_space=pl.ANY),
            pl.BlockSpec(memory_space=pltpu.VMEM),
        ],
        out_shape=[
            jax.ShapeDtypeStruct((owned * labels, width), bf16),
            jax.ShapeDtypeStruct((rows, width), bf16),
        ],
        scratch_shapes=[
            pltpu.VMEM((owned * labels, width), bf16),
            pltpu.VMEM((8, block, packed), bf16),
            pltpu.VMEM((8, block, owned * labels), bf16),
            pltpu.VMEM((8, block, width), bf16),
            pltpu.VMEM((4, block, width), bf16),
            pltpu.VMEM((2, block, width), bf16),
            pltpu.VMEM((block, width), bf16),
            pltpu.VMEM((ZS - 1, rows, width), bf16),
            pltpu.VMEM((count, labels // 2, width), bf16),
            pltpu.SemaphoreType.DMA((47,)),
            pltpu.SemaphoreType.DMA((47,)),
            pltpu.SemaphoreType.DMA,
            pltpu.SemaphoreType.DMA((count,)),
        ],
        compiler_params=pltpu.CompilerParams(
            collective_id=0, has_side_effects=True, vmem_limit_bytes=60 * 1024 * 1024
        ),
    )(
        queries,
        shortlist.T,
        pos_rank.T,
        pos_label.T,
        weights.reshape(owned * labels, width),
    )


def body(queries, weights, shortlist, pos_rank, pos_label):
    rows, width = queries.shape
    owned, labels, _ = weights.shape
    pb_count, col_count = lax.axis_size("pb"), lax.axis_size("col")
    devices = pb_count * col_count
    if (pb_count, col_count) == (4, 2 * ZS):
        grad_weights, grad_queries = routed(queries, weights, shortlist, pos_rank, pos_label)
        return grad_weights.reshape(weights.shape), grad_queries
    sent = jnp.concatenate([queries, query_meta(shortlist, pos_rank, pos_label)], axis=1)
    everyone = lax.all_gather(sent, ("pb", "col"), axis=0, tiled=True)
    total = devices * rows
    block = 256
    grad_weights, part = pl.pallas_call(
        functools.partial(dense_kernel, owned, labels, shortlist.shape[1], pos_rank.shape[1]),
        grid=(total // block,),
        in_specs=[
            pl.BlockSpec((block, width), lambda i: (i, 0)),
            pl.BlockSpec((block, META), lambda i: (i, width // META)),
            pl.BlockSpec((owned * labels, width), lambda i: (0, 0)),
        ],
        out_specs=[
            pl.BlockSpec((owned * labels, width), lambda i: (0, 0)),
            pl.BlockSpec((block, width), lambda i: (i, 0)),
        ],
        out_shape=[
            jax.ShapeDtypeStruct((owned * labels, width), jnp.bfloat16),
            jax.ShapeDtypeStruct((total, width), jnp.bfloat16),
        ],
        scratch_shapes=[pltpu.VMEM((owned * labels, width), jnp.float32)],
        compiler_params=pltpu.CompilerParams(vmem_limit_bytes=60 * 1024 * 1024),
    )(everyone, everyone, weights.reshape(owned * labels, width))
    part = part.reshape(pb_count, col_count, rows, width)
    part = lax.all_to_all(part, "pb", split_axis=0, concat_axis=0, tiled=True)
    part = jnp.sum(part, axis=0, dtype=jnp.float32).astype(jnp.bfloat16)
    part = lax.all_to_all(part, "col", split_axis=0, concat_axis=0, tiled=True)
    grad_queries = jnp.sum(part, axis=0, dtype=jnp.float32).astype(jnp.bfloat16)
    return grad_weights.reshape(weights.shape), grad_queries


def solution(mesh):
    return jax.shard_map(
        body,
        mesh=mesh,
        in_specs=(
            P(("pb", "col"), None),
            P(("pb", "col"), None, None),
            P(("pb", "col"), None),
            P(("pb", "col"), None),
            P(("pb", "col"), None),
        ),
        out_specs=(P(("pb", "col"), None, None), P(("pb", "col"), None)),
        check_vma=False,
    )
```
